32 devices in a mesh: seq: 8 (over y, x, core), head: 4 (over z).
Axes of the slice: x: 2, y: 2, z: 4, core: 2. Of those that a mesh axis runs over, the one named last changes fastest.
Arguments:
- queries: bfloat16 [8192, 32, 128], P(('seq', 'head')), may hold values from -6 to 6
- keys: bfloat16 [8192, 32, 2, 128], P(('seq', 'head')), may hold values from -6 to 6
- values: bfloat16 [8192, 32, 2, 128], P(('seq', 'head')), may hold values from -6 to 6
- initial_state: float32 [32, 128, 128], P('head'), may hold values from -192 to 192
Outputs:
- mixed: bfloat16 [8192, 32, 128], P(('seq', 'head'))
The draws below stay inside these ranges and needn't reach their ends.
All inputs are finite; a program needn't handle non-finite values.
Results may differ from the reference program's by a relative error of at most 0.004.
Values may be sent and summed in bfloat16 or wider, within the bound.
A program may use at most 128 MiB of HBM per device.

```python
import jax
import jax.numpy as jnp
from jax import lax

HD = 128
HEADS = 32
UPDATES = 2
TOKENS = 8192


def shard_levels(own_key, dims, shards, smallest, top_value):
    def one(axis_at, shards_of):
        heights = jax.random.uniform(jax.random.fold_in(jax.random.fold_in(own_key, 6), axis_at), (shards_of,), jnp.float32, smallest / len(shards), top_value / len(shards))
        return jnp.repeat(jnp.exp(heights), dims[axis_at] // shards_of).reshape((-1,) + (1,) * (len(dims) - axis_at - 1))

    level = one(*shards[0])
    for cut in shards[1:]:
        level = level * one(*cut)
    return level


def gaussian(rng, extent, scale, bound, split=(), dtype=jnp.bfloat16):
    entries = scale * jax.random.normal(rng, extent, jnp.float32)
    if split:
        entries = entries * shard_levels(rng, extent, split, -0.22, 0.18)
    return jnp.clip(entries, -bound, bound).astype(dtype)


def setup_inputs(seed: int = 0) -> dict:
    arg_keys = jax.random.split(jax.random.key(seed), 5)
    return {
        "queries": gaussian(arg_keys[0], (TOKENS, HEADS, HD), 1.0, 6.0, ((0, 32),)),
        "keys": gaussian(arg_keys[1], (TOKENS, HEADS, UPDATES, HD), 1.0, 6.0, ((0, 32),)),
        "values": gaussian(arg_keys[2], (TOKENS, HEADS, UPDATES, HD), 1.0, 6.0, ((0, 32),)),
        "initial_state": gaussian(arg_keys[3], (HEADS, HD, HD), 32.0, 192.0, ((0, 4),), jnp.float32),
    }


HIGH = lax.Precision.HIGHEST

def unit_rows(raw_keys):
    floats = raw_keys.astype(jnp.float32)
    return floats * lax.rsqrt(lax.optimization_barrier(jnp.sum(floats * floats, axis=-1, keepdims=True)) + 1e-06)

def reference(queries, keys, values, initial_state):
    q_float = queries.astype(jnp.float32)
    k_unit = unit_rows(keys)
    v_float = values.astype(jnp.float32)

    def advance(carry_state, token_item):
        q_now, k_now, v_now = token_item
        for index_j in range(UPDATES):
            key_now = k_now[:, index_j]
            projected = jnp.einsum('hd,hde->he', key_now, carry_state, precision=HIGH)
            carry_state = carry_state + 2.0 * key_now[:, :, None] * (v_now[:, index_j] - projected)[:, None, :]
        return (carry_state, jnp.einsum('hd,hde->he', q_now, carry_state, precision=HIGH))
    final_state, raw_out = lax.scan(advance, initial_state.astype(jnp.float32), (q_float, k_unit, v_float))
    scaled = raw_out * lax.rsqrt(lax.optimization_barrier(jnp.mean(raw_out * raw_out, axis=-1, keepdims=True)) + 1e-06)
    return scaled.astype(jnp.bfloat16)
```

```python
import functools

import jax
import jax.numpy as jnp
from jax import lax
from jax.experimental import pallas as pl
from jax.experimental.pallas import tpu as pltpu
from jax.sharding import PartitionSpec as P

BLOCK = 64
BASE = 16
HEADS_A_STEP = 1
INBOX_BYTES = 24 << 20

F32 = jnp.float32
BF16 = jnp.bfloat16
MESH = pl.DeviceIdType.MESH


def mm(left, right, dims=((1,), (0,))):
    return lax.dot_general(left, right, (dims, ((), ())), preferred_element_type=F32)


def split(x):
    high = x.astype(BF16)
    return high, (x - high.astype(F32)).astype(BF16)


def cat(parts, axis):
    return jnp.concatenate(parts, axis=axis)


def exact_left(left, right):
    high, low = split(right)
    return mm(cat([left, left], 1), cat([high, low], 0))


def exact_right(left, right):
    high, low = split(left)
    return mm(cat([high, low], 1), cat([right, right], 0))


def both_split(lh, ll, rh, rl):
    return mm(cat([lh, ll], 1), cat([rh, rh], 0)) + mm(lh, rl)


def both(left, right):
    return both_split(*split(left), *split(right))


def odd_rows(x, size):
    rows = x.shape[0]
    return cat([x[s : s + size] for s in range(size, rows, 2 * size)], 0)


def merge_rows(even_from, odd, size):
    rows = even_from.shape[0]
    parts = []
    for i, s in enumerate(range(0, rows, 2 * size)):
        parts += [even_from[s : s + size], odd[i * size : (i + 1) * size]]
    return cat(parts, 0)


def unit_lower_inverse(x):
    n = x.shape[0]
    row = lax.broadcasted_iota(jnp.int32, (n, n), 0)
    col = lax.broadcasted_iota(jnp.int32, (n, n), 1)
    same = row // BASE == col // BASE
    inner = jnp.where(same, x, 0.0)
    packed = inner[:BASE]
    for s in range(BASE, n, BASE):
        packed = packed + inner[s : s + BASE]
    sub = lax.broadcasted_iota(jnp.int32, (BASE, n), 0)
    lane = lax.broadcasted_iota(jnp.int32, (BASE, n), 1)
    inv = jnp.where(sub == lane % BASE, 1.0, 0.0)
    for j in range(BASE - 1):
        coef = jnp.take_along_axis(packed, lane - lane % BASE + j, axis=1)
        inv = inv - coef * inv[j : j + 1]
    m = jnp.where(same, cat([inv] * (n // BASE), 0), 0.0)
    size = BASE
    while size < n:
        below = odd_rows(jnp.where(col // size == row // size - 1, x, 0.0), size)
        mh, ml = split(m)
        y = both_split(*split(below), mh, ml)
        y = merge_rows(jnp.zeros((n, n), F32), y, size)
        z = both_split(odd_rows(mh, size), odd_rows(ml, size), *split(y))
        m = merge_rows(m, odd_rows(m, size) - z, size)
        size *= 2
    return m


def block_factors(q, k, v):
    n, width = k.shape
    tokens = q.shape[0]
    kq = cat([k, q], 0)
    gs = mm(kq, k, ((1,), (1,)))
    gram, scores = gs[:n], gs[n:]
    row = lax.broadcasted_iota(jnp.int32, (n, n), 0)
    col = lax.broadcasted_iota(jnp.int32, (n, n), 1)
    diag = jnp.where(row == col, gram, 0.0)
    d_col = lax.rsqrt(jnp.sum(diag, axis=1, keepdims=True) + 1e-06)
    d_row = lax.rsqrt(jnp.sum(diag, axis=0, keepdims=True) + 1e-06)
    x = jnp.where(col < row, (2.0 * d_col) * gram * d_row, 0.0)
    scaled = unit_lower_inverse(x) * (2.0 * d_col)
    trow = lax.broadcasted_iota(jnp.int32, (tokens, n), 0)
    tcol = lax.broadcasted_iota(jnp.int32, (tokens, n), 1)
    seen = jnp.where(tcol < (trow + 1) * (n // tokens), scores, 0.0)
    return kq, scaled * d_row, exact_right(scaled, v), seen


def local_kernel(q_ref, k_ref, v_ref, pair_ref, local_ref, gain_ref):
    heads, tokens, width = q_ref.shape
    per_token = k_ref.shape[1] // tokens
    step = min(BLOCK, tokens)
    n = step * per_token
    for h in range(heads):
        factors = []
        for b in range(tokens // step):
            k = k_ref[h, b * n : (b + 1) * n]
            q = q_ref[h, b * step : (b + 1) * step]
            v = v_ref[h, b * n : (b + 1) * n]
            factors.append((k,) + block_factors(q, k, v))
        row = lax.broadcasted_iota(jnp.int32, (width, width), 0)
        col = lax.broadcasted_iota(jnp.int32, (width, width), 1)
        eye = jnp.where(row == col, 1.0, 0.0)
        pair = cat([jnp.zeros((width, width), F32), eye], 1)
        for b, (k, kq, near, fed, seen) in enumerate(factors):
            if b == 0:
                q = kq[n:].astype(F32)
                passed = cat([jnp.zeros_like(q), q], 1)
                feed = cat([fed, -exact_right(near, k)], 1)
            else:
                ahead = exact_left(kq, pair)
                passed = ahead[n:]
                feed = cat([fed, jnp.zeros_like(fed)], 1) - both(near, ahead[:n])
            fh, fl = split(feed)
            out = passed + both_split(*split(seen), fh, fl)
            pair = pair + mm(cat([k, k], 0), cat([fh, fl], 0), ((0,), (0,)))
            local_ref[h, b * step : (b + 1) * step] = out[:, :width]
            gain_ref[h, b * step : (b + 1) * step] = out[:, width:]
        pair_ref[h] = pair


def local_pass(q, k, v):
    heads, tokens, width = q.shape
    g = HEADS_A_STEP

    def spec(rows, columns):
        return pl.BlockSpec((g, rows, columns), lambda i: (i, 0, 0))

    return pl.pallas_call(
        local_kernel,
        grid=(heads // g,),
        in_specs=[spec(tokens, width), spec(k.shape[1], width), spec(k.shape[1], width)],
        out_specs=[spec(width, 2 * width), spec(tokens, width), spec(tokens, width)],
        out_shape=[
            jax.ShapeDtypeStruct((heads, width, 2 * width), F32),
            jax.ShapeDtypeStruct((heads, tokens, width), F32),
            jax.ShapeDtypeStruct((heads, tokens, width), F32),
        ],
        name="local_pass",
    )(q, k, v)


def relay_kernel(
    ns, nh, pair_ref, init_ref, sin_ref, inbox, states, send, recv, send_state, recv_state
):
    si, zi = lax.axis_index("seq"), lax.axis_index("head")
    me = si * nh + zi
    n = ns * nh
    mine = zi * ns + si
    width = init_ref.shape[1]

    def place(p):
        return p // nh, lax.rem(p, nh)

    barrier = pltpu.get_barrier_semaphore()

    @pl.loop(1, n)
    def _(i):
        pl.semaphore_signal(
            barrier, inc=1, device_id=place(lax.rem(me + i, n)), device_id_type=MESH
        )

    pl.semaphore_wait(barrier, n - 1)

    def pair_copy(i):
        ps, pz = place(lax.rem(me + i, n))
        return pltpu.make_async_remote_copy(
            src_ref=pair_ref.at[pz * ns + ps],
            dst_ref=inbox.at[me],
            send_sem=send.at[i],
            recv_sem=recv.at[me],
            device_id=(ps, pz),
            device_id_type=MESH,
        )

    def state_copy(d):
        return pltpu.make_async_remote_copy(
            src_ref=states.at[d],
            dst_ref=sin_ref.at[mine],
            send_sem=send_state.at[d],
            recv_sem=recv_state.at[mine],
            device_id=place(d),
            device_id_type=MESH,
        )

    @pl.loop(1, n)
    def _(i):
        pair_copy(i).start()

    pltpu.make_async_copy(pair_ref.at[mine], inbox.at[me], recv.at[me]).start()

    def advance(d, state):
        states[d] = state.astype(states.dtype)

        @pl.when(d != me)
        def _():
            state_copy(d).start()

        @pl.when(d == me)
        def _():
            pltpu.make_async_copy(states.at[d], sin_ref.at[mine], recv_state.at[mine]).start()

        pltpu.make_async_copy(inbox.at[d], inbox.at[d], recv.at[d]).wait()
        pair = inbox[d]
        return both(pair[:, width:], state) + pair[:, :width]

    lax.fori_loop(0, n, advance, init_ref[si])

    @pl.loop(1, n)
    def _(i):
        pair_copy(i).wait_send()

    @pl.loop(0, n)
    def _(d):
        @pl.when(d != me)
        def _():
            state_copy(d).wait_send()

    @pl.loop(0, n)
    def _(h):
        pltpu.make_async_copy(sin_ref.at[h], sin_ref.at[h], recv_state.at[h]).wait()


def relay(pairs, initial_state):
    ns, nh = lax.axis_size("seq"), lax.axis_size("head")
    n = ns * nh
    heads, width, _ = pairs.shape
    return pl.pallas_call(
        functools.partial(relay_kernel, ns, nh),
        in_specs=[pl.BlockSpec(memory_space=pl.ANY), pl.BlockSpec(memory_space=pltpu.VMEM)],
        out_specs=pl.BlockSpec(memory_space=pl.ANY),
        out_shape=jax.ShapeDtypeStruct((heads, width, width), F32),
        scratch_shapes=[
            pltpu.VMEM((n, width, 2 * width), F32),
            pltpu.VMEM((n, width, width), F32),
            pltpu.SemaphoreType.DMA((n,)),
            pltpu.SemaphoreType.DMA((n,)),
            pltpu.SemaphoreType.DMA((n,)),
            pltpu.SemaphoreType.DMA((heads,)),
        ],
        compiler_params=pltpu.CompilerParams(collective_id=0, has_side_effects=True),
        name="relay",
    )(pairs, initial_state)


def finish_kernel(local_ref, gain_ref, state_ref, out_ref):
    for h in range(local_ref.shape[0]):
        raw = local_ref[h] + both(gain_ref[h], state_ref[h])
        mean = jnp.mean(raw * raw, axis=-1, keepdims=True)
        out_ref[h] = (raw * lax.rsqrt(mean + 1e-06)).astype(out_ref.dtype)


def finish(local, gain, state):
    heads, tokens, width = local.shape
    g = 4 if heads % 4 == 0 else 1

    def spec(rows):
        return pl.BlockSpec((g, rows, width), lambda i: (i, 0, 0))

    return pl.pallas_call(
        finish_kernel,
        grid=(heads // g,),
        in_specs=[spec(tokens), spec(tokens), spec(width)],
        out_specs=spec(tokens),
        out_shape=jax.ShapeDtypeStruct((heads, tokens, width), BF16),
        name="finish",
    )(local, gain, state)


def owned_per_device(queries, keys, values, initial_state):
    tokens, heads, width = queries.shape
    q = jnp.swapaxes(queries, 0, 1)
    k = jnp.moveaxis(keys, 1, 0).reshape(heads, -1, width)
    v = jnp.moveaxis(values, 1, 0).reshape(heads, -1, width)
    pairs, local, gain = local_pass(q, k, v)
    incoming = relay(pairs, initial_state)
    return jnp.swapaxes(finish(local, gain, incoming), 0, 1)


HIGH = lax.Precision.HIGHEST


def shifted(value, axis, by):
    size = lax.axis_size(axis)
    pairs = [(i, i + by) for i in range(size) if 0 <= i + by < size]
    return lax.ppermute(value, axis, pairs)


def matmul(left, right):
    return jnp.dot(left, right, precision=HIGH, preferred_element_type=jnp.float32)


def batched(left, right):
    return jnp.einsum("hij,hjk->hik", left, right, precision=HIGH)


def unit_rows(raw_keys):
    floats = raw_keys.astype(jnp.float32)
    return floats * lax.rsqrt(jnp.sum(floats * floats, axis=-1, keepdims=True) + 1e-06)


def all_factors(k_blocks, v_blocks):
    updates = k_blocks.shape[2]
    head_width = k_blocks.shape[3]
    gram = jnp.einsum("hbid,hbjd->hbij", k_blocks, k_blocks, precision=HIGH)
    system = jnp.eye(updates, dtype=jnp.float32) + jnp.tril(2.0 * gram, -1)
    solved = lax.linalg.triangular_solve(
        system,
        2.0 * jnp.concatenate([k_blocks, v_blocks], axis=-1),
        left_side=True,
        lower=True,
        unit_diagonal=True,
    )
    return (solved[..., :head_width], solved[..., head_width:])


def visible_scores(q_blk, k_blk):
    rows = q_blk.shape[0]
    updates = k_blk.shape[0]
    per_token = updates // rows
    row_ids = lax.broadcasted_iota(jnp.int32, (rows, updates), 0)
    col_ids = lax.broadcasted_iota(jnp.int32, (rows, updates), 1)
    return jnp.where(col_ids < (row_ids + 1) * per_token, matmul(q_blk, k_blk.T), 0.0)


def start_pair(head_width):
    return jnp.concatenate(
        [jnp.zeros((head_width, head_width), jnp.float32), jnp.eye(head_width, dtype=jnp.float32)],
        axis=1,
    )


def carried_pass(q_blocks, k_blocks, w_blocks, u_blocks):
    head_width = q_blocks.shape[2]

    def advance(pair_state, block_item):
        q_blk, k_blk, w_mat, u_mat = block_item
        feed_rows = jnp.concatenate([u_mat, jnp.zeros_like(u_mat)], axis=1) - matmul(
            w_mat, pair_state
        )
        outputs = matmul(q_blk, pair_state) + matmul(visible_scores(q_blk, k_blk), feed_rows)
        return (pair_state + matmul(k_blk.T, feed_rows), outputs)

    final_pair, outputs = lax.scan(
        advance, start_pair(head_width), (q_blocks, k_blocks, w_blocks, u_blocks)
    )
    outputs = outputs.reshape(-1, 2 * head_width)
    return (
        final_pair[:, head_width:],
        final_pair[:, :head_width],
        outputs[:, :head_width],
        outputs[:, head_width:],
    )


def per_device(queries, keys, values, initial_state):
    q_heads, k_heads, v_heads = (
        lax.all_to_all(queries, "head", split_axis=1, concat_axis=0, tiled=True),
        lax.all_to_all(keys, "head", split_axis=1, concat_axis=0, tiled=True),
        lax.all_to_all(values, "head", split_axis=1, concat_axis=0, tiled=True),
    )
    head_width = q_heads.shape[2]
    local_heads = q_heads.shape[1]
    blocks = q_heads.shape[0] // BLOCK
    q_blocks = jnp.moveaxis(q_heads.astype(jnp.float32), 1, 0).reshape(
        local_heads, blocks, BLOCK, head_width
    )
    k_blocks = jnp.moveaxis(unit_rows(k_heads), 1, 0).reshape(local_heads, blocks, -1, head_width)
    v_blocks = jnp.moveaxis(v_heads.astype(jnp.float32), 1, 0).reshape(
        local_heads, blocks, -1, head_width
    )
    w_blocks, u_blocks = all_factors(k_blocks, v_blocks)
    transition, additive, local_out, query_gain = jax.vmap(carried_pass)(
        q_blocks, k_blocks, w_blocks, u_blocks
    )
    at_first = lax.axis_index("seq") == 0
    start_state = jnp.where(at_first, initial_state, jnp.zeros_like(initial_state))

    def relay_step(loop_step, current):
        passed = shifted(batched(transition, current) + additive, "seq", 1)
        return jnp.where(at_first, initial_state, passed)

    incoming = lax.fori_loop(0, lax.axis_size("seq") - 1, relay_step, start_state)
    raw_out = local_out + batched(query_gain, incoming)
    scaled = raw_out * lax.rsqrt(jnp.mean(raw_out * raw_out, axis=-1, keepdims=True) + 1e-06)
    tokens_major = jnp.moveaxis(scaled.astype(jnp.bfloat16), 0, 1)
    return lax.all_to_all(tokens_major, "head", split_axis=0, concat_axis=1, tiled=True)


def solution(mesh):
    placed = (
        P(("seq", "head"), None, None),
        P(("seq", "head"), None, None, None),
        P(("seq", "head"), None, None, None),
        P("head", None, None),
    )
    devices = mesh.shape["seq"] * mesh.shape["head"]

    def chosen(queries, keys, values, initial_state):
        own_heads, width = initial_state.shape[:2]
        inbox = devices * 2 * width * width * 4
        if own_heads == mesh.shape["seq"] and inbox <= INBOX_BYTES:
            return owned_per_device(queries, keys, values, initial_state)
        return per_device(queries, keys, values, initial_state)

    return jax.shard_map(
        chosen,
        mesh=mesh,
        in_specs=placed,
        out_specs=P(("seq", "head"), None, None),
        check_vma=False,
    )
```

```python
import functools

import jax
import jax.numpy as jnp
from jax import lax
from jax.experimental import pallas as pl
from jax.experimental.pallas import tpu as pltpu
from jax.sharding import PartitionSpec as P

BLOCK = 64
BASE = 16
HEADS_A_STEP = 4
INBOX_BYTES = 24 << 20

F32 = jnp.float32
BF16 = jnp.bfloat16
MESH = pl.DeviceIdType.MESH


def mm(left, right, dims=((1,), (0,))):
    return lax.dot_general(left, right, (dims, ((), ())), preferred_element_type=F32)


def split(x):
    high = x.astype(BF16)
    return high, (x - high.astype(F32)).astype(BF16)


def cat(parts, axis):
    return jnp.concatenate(parts, axis=axis)


def exact_left(left, right):
    high, low = split(right)
    return mm(cat([left, left], 1), cat([high, low], 0))


def exact_right(left, right):
    high, low = split(left)
    return mm(cat([high, low], 1), cat([right, right], 0))


def both_split(lh, ll, rh, rl):
    return mm(cat([lh, ll], 1), cat([rh, rh], 0)) + mm(lh, rl)


def both(left, right):
    return both_split(*split(left), *split(right))


def odd_rows(x, size):
    rows = x.shape[0]
    return cat([x[s : s + size] for s in range(size, rows, 2 * size)], 0)


def merge_rows(even_from, odd, size):
    rows = even_from.shape[0]
    parts = []
    for i, s in enumerate(range(0, rows, 2 * size)):
        parts += [even_from[s : s + size], odd[i * size : (i + 1) * size]]
    return cat(parts, 0)


def unit_lower_inverses(xs):
    n = xs[0].shape[0]
    row = lax.broadcasted_iota(jnp.int32, (n, n), 0)
    col = lax.broadcasted_iota(jnp.int32, (n, n), 1)
    same = row // BASE == col // BASE
    sub = lax.broadcasted_iota(jnp.int32, (BASE, n), 0)
    lane = lax.broadcasted_iota(jnp.int32, (BASE, n), 1)
    packs = []
    for x in xs:
        inner = jnp.where(same, x, 0.0)
        packed = inner[:BASE]
        for s in range(BASE, n, BASE):
            packed = packed + inner[s : s + BASE]
        packs.append(packed)
    invs = [jnp.where(sub == lane % BASE, 1.0, 0.0) for _ in xs]
    for j in range(BASE - 1):
        at = lane - lane % BASE + j
        coefs = [jnp.take_along_axis(packed, at, axis=1) for packed in packs]
        invs = [inv - coef * inv[j : j + 1] for inv, coef in zip(invs, coefs)]
    ms = [jnp.where(same, cat([inv] * (n // BASE), 0), 0.0) for inv in invs]
    size = BASE
    while size < n:
        near = col // size == row // size - 1
        belows = [split(odd_rows(jnp.where(near, x, 0.0), size)) for x in xs]
        halves = [split(m) for m in ms]
        ys = [both_split(*below, *half) for below, half in zip(belows, halves)]
        ys = [split(merge_rows(jnp.zeros((n, n), F32), y, size)) for y in ys]
        zs = [
            both_split(odd_rows(mh, size), odd_rows(ml, size), *y)
            for (mh, ml), y in zip(halves, ys)
        ]
        ms = [merge_rows(m, odd_rows(m, size) - z, size) for m, z in zip(ms, zs)]
        size *= 2
    return ms


def block_factors(blocks):
    n, width = blocks[0][1].shape
    tokens = blocks[0][0].shape[0]
    row = lax.broadcasted_iota(jnp.int32, (n, n), 0)
    col = lax.broadcasted_iota(jnp.int32, (n, n), 1)
    trow = lax.broadcasted_iota(jnp.int32, (tokens, n), 0)
    tcol = lax.broadcasted_iota(jnp.int32, (tokens, n), 1)
    visible = tcol < (trow + 1) * (n // tokens)
    kqs = [cat([k, q], 0) for q, k, _ in blocks]
    products = [mm(kq, k, ((1,), (1,))) for kq, (_, k, _) in zip(kqs, blocks)]
    xs, d_cols, d_rows, seens = [], [], [], []
    for gs in products:
        gram = gs[:n]
        diag = jnp.where(row == col, gram, 0.0)
        d_col = lax.rsqrt(jnp.sum(diag, axis=1, keepdims=True) + 1e-06)
        d_row = lax.rsqrt(jnp.sum(diag, axis=0, keepdims=True) + 1e-06)
        xs.append(jnp.where(col < row, (2.0 * d_col) * gram * d_row, 0.0))
        d_cols.append(d_col)
        d_rows.append(d_row)
        seens.append(split(jnp.where(visible, gs[n:], 0.0)))
    scaled = [m * (2.0 * d_col) for m, d_col in zip(unit_lower_inverses(xs), d_cols)]
    feds = [exact_right(m, v) for m, (_, _, v) in zip(scaled, blocks)]
    nears = [split(m * d_row) for m, d_row in zip(scaled, d_rows)]
    return kqs, nears, feds, seens


def local_kernel(q_ref, k_ref, v_ref, pair_ref, local_ref, gain_ref):
    heads, tokens, width = q_ref.shape
    per_token = k_ref.shape[1] // tokens
    step = min(BLOCK, tokens)
    n = step * per_token
    count = tokens // step
    blocks = [
        (
            q_ref[h, b * step : (b + 1) * step],
            k_ref[h, b * n : (b + 1) * n],
            v_ref[h, b * n : (b + 1) * n],
        )
        for b in range(count)
        for h in range(heads)
    ]
    kqs, nears, feds, seens = block_factors(blocks)
    row = lax.broadcasted_iota(jnp.int32, (width, width), 0)
    col = lax.broadcasted_iota(jnp.int32, (width, width), 1)
    eye = jnp.where(row == col, 1.0, 0.0)
    pairs = [cat([jnp.zeros((width, width), F32), eye], 1)] * heads
    for b in range(count):
        at = slice(b * heads, (b + 1) * heads)
        if b == 0:
            qs = [kq[n:].astype(F32) for kq in kqs[at]]
            passed = [cat([jnp.zeros_like(q), q], 1) for q in qs]
            feeds = [
                cat([fed, -mm(cat(list(near), 1), cat([kq[:n], kq[:n]], 0))], 1)
                for fed, near, kq in zip(feds[at], nears[at], kqs[at])
            ]
        else:
            aheads = [exact_left(kq, pair) for kq, pair in zip(kqs[at], pairs)]
            passed = [ahead[n:] for ahead in aheads]
            feeds = [
                cat([fed, jnp.zeros_like(fed)], 1) - both_split(*near, *split(ahead[:n]))
                for fed, near, ahead in zip(feds[at], nears[at], aheads)
            ]
        feeds = [split(feed) for feed in feeds]
        pairs = [
            pair + mm(cat([kq[:n], kq[:n]], 0), cat(list(feed), 0), ((0,), (0,)))
            for pair, kq, feed in zip(pairs, kqs[at], feeds)
        ]
        outs = [
            base + both_split(*seen, *feed)
            for base, seen, feed in zip(passed, seens[at], feeds)
        ]
        for h, out in enumerate(outs):
            local_ref[h, b * step : (b + 1) * step] = out[:, :width]
            gain_ref[h, b * step : (b + 1) * step] = out[:, width:]
    for h, pair in enumerate(pairs):
        pair_ref[h] = pair


def local_pass(q, k, v):
    heads, tokens, width = q.shape
    g = HEADS_A_STEP

    def spec(rows, columns):
        return pl.BlockSpec((g, rows, columns), lambda i: (i, 0, 0))

    return pl.pallas_call(
        local_kernel,
        grid=(heads // g,),
        in_specs=[spec(tokens, width), spec(k.shape[1], width), spec(k.shape[1], width)],
        out_specs=[spec(width, 2 * width), spec(tokens, width), spec(tokens, width)],
        out_shape=[
            jax.ShapeDtypeStruct((heads, width, 2 * width), F32),
            jax.ShapeDtypeStruct((heads, tokens, width), F32),
            jax.ShapeDtypeStruct((heads, tokens, width), F32),
        ],
        name="local_pass",
    )(q, k, v)


def relay_kernel(
    ns, nh, pair_ref, init_ref, sin_ref, inbox, states, send, recv, send_state, recv_state
):
    si, zi = lax.axis_index("seq"), lax.axis_index("head")
    me = si * nh + zi
    n = ns * nh
    mine = zi * ns + si
    width = init_ref.shape[1]

    def place(p):
        return p // nh, lax.rem(p, nh)

    barrier = pltpu.get_barrier_semaphore()

    @pl.loop(1, n)
    def _(i):
        pl.semaphore_signal(
            barrier, inc=1, device_id=place(lax.rem(me + i, n)), device_id_type=MESH
        )

    pl.semaphore_wait(barrier, n - 1)

    def pair_copy(i):
        ps, pz = place(lax.rem(me + i, n))
        return pltpu.make_async_remote_copy(
            src_ref=pair_ref.at[pz * ns + ps],
            dst_ref=inbox.at[me],
            send_sem=send.at[i],
            recv_sem=recv.at[me],
            device_id=(ps, pz),
            device_id_type=MESH,
        )

    def state_copy(d):
        return pltpu.make_async_remote_copy(
            src_ref=states.at[d],
            dst_ref=sin_ref.at[mine],
            send_sem=send_state.at[d],
            recv_sem=recv_state.at[mine],
            device_id=place(d),
            device_id_type=MESH,
        )

    @pl.loop(1, n)
    def _(i):
        pair_copy(i).start()

    pltpu.make_async_copy(pair_ref.at[mine], inbox.at[me], recv.at[me]).start()

    def advance(d, state):
        states[d] = state.astype(states.dtype)

        @pl.when(d != me)
        def _():
            state_copy(d).start()

        @pl.when(d == me)
        def _():
            pltpu.make_async_copy(states.at[d], sin_ref.at[mine], recv_state.at[mine]).start()

        pltpu.make_async_copy(inbox.at[d], inbox.at[d], recv.at[d]).wait()
        pair = inbox[d]
        return both(pair[:, width:], state) + pair[:, :width]

    lax.fori_loop(0, n, advance, init_ref[si])

    @pl.loop(1, n)
    def _(i):
        pair_copy(i).wait_send()

    @pl.loop(0, n)
    def _(d):
        @pl.when(d != me)
        def _():
            state_copy(d).wait_send()

    @pl.loop(0, n)
    def _(h):
        pltpu.make_async_copy(sin_ref.at[h], sin_ref.at[h], recv_state.at[h]).wait()


def relay(pairs, initial_state):
    ns, nh = lax.axis_size("seq"), lax.axis_size("head")
    n = ns * nh
    heads, width, _ = pairs.shape
    return pl.pallas_call(
        functools.partial(relay_kernel, ns, nh),
        in_specs=[pl.BlockSpec(memory_space=pl.ANY), pl.BlockSpec(memory_space=pltpu.VMEM)],
        out_specs=pl.BlockSpec(memory_space=pl.ANY),
        out_shape=jax.ShapeDtypeStruct((heads, width, width), F32),
        scratch_shapes=[
            pltpu.VMEM((n, width, 2 * width), F32),
            pltpu.VMEM((n, width, width), F32),
            pltpu.SemaphoreType.DMA((n,)),
            pltpu.SemaphoreType.DMA((n,)),
            pltpu.SemaphoreType.DMA((n,)),
            pltpu.SemaphoreType.DMA((heads,)),
        ],
        compiler_params=pltpu.CompilerParams(collective_id=0, has_side_effects=True),
        name="relay",
    )(pairs, initial_state)


def finish_kernel(local_ref, gain_ref, state_ref, out_ref):
    for h in range(local_ref.shape[0]):
        raw = local_ref[h] + both(gain_ref[h], state_ref[h])
        mean = jnp.mean(raw * raw, axis=-1, keepdims=True)
        out_ref[h] = (raw * lax.rsqrt(mean + 1e-06)).astype(out_ref.dtype)


def finish(local, gain, state):
    heads, tokens, width = local.shape
    g = 4 if heads % 4 == 0 else 1

    def spec(rows):
        return pl.BlockSpec((g, rows, width), lambda i: (i, 0, 0))

    return pl.pallas_call(
        finish_kernel,
        grid=(heads // g,),
        in_specs=[spec(tokens), spec(tokens), spec(width)],
        out_specs=spec(tokens),
        out_shape=jax.ShapeDtypeStruct((heads, tokens, width), BF16),
        name="finish",
    )(local, gain, state)


def owned_per_device(queries, keys, values, initial_state):
    tokens, heads, width = queries.shape
    q = jnp.swapaxes(queries, 0, 1)
    k = jnp.moveaxis(keys, 1, 0).reshape(heads, -1, width)
    v = jnp.moveaxis(values, 1, 0).reshape(heads, -1, width)
    pairs, local, gain = local_pass(q, k, v)
    incoming = relay(pairs, initial_state)
    return jnp.swapaxes(finish(local, gain, incoming), 0, 1)


HIGH = lax.Precision.HIGHEST


def shifted(value, axis, by):
    size = lax.axis_size(axis)
    pairs = [(i, i + by) for i in range(size) if 0 <= i + by < size]
    return lax.ppermute(value, axis, pairs)


def matmul(left, right):
    return jnp.dot(left, right, precision=HIGH, preferred_element_type=jnp.float32)


def batched(left, right):
    return jnp.einsum("hij,hjk->hik", left, right, precision=HIGH)


def unit_rows(raw_keys):
    floats = raw_keys.astype(jnp.float32)
    return floats * lax.rsqrt(jnp.sum(floats * floats, axis=-1, keepdims=True) + 1e-06)


def all_factors(k_blocks, v_blocks):
    updates = k_blocks.shape[2]
    head_width = k_blocks.shape[3]
    gram = jnp.einsum("hbid,hbjd->hbij", k_blocks, k_blocks, precision=HIGH)
    system = jnp.eye(updates, dtype=jnp.float32) + jnp.tril(2.0 * gram, -1)
    solved = lax.linalg.triangular_solve(
        system,
        2.0 * jnp.concatenate([k_blocks, v_blocks], axis=-1),
        left_side=True,
        lower=True,
        unit_diagonal=True,
    )
    return (solved[..., :head_width], solved[..., head_width:])


def visible_scores(q_blk, k_blk):
    rows = q_blk.shape[0]
    updates = k_blk.shape[0]
    per_token = updates // rows
    row_ids = lax.broadcasted_iota(jnp.int32, (rows, updates), 0)
    col_ids = lax.broadcasted_iota(jnp.int32, (rows, updates), 1)
    return jnp.where(col_ids < (row_ids + 1) * per_token, matmul(q_blk, k_blk.T), 0.0)


def start_pair(head_width):
    return jnp.concatenate(
        [jnp.zeros((head_width, head_width), jnp.float32), jnp.eye(head_width, dtype=jnp.float32)],
        axis=1,
    )


def carried_pass(q_blocks, k_blocks, w_blocks, u_blocks):
    head_width = q_blocks.shape[2]

    def advance(pair_state, block_item):
        q_blk, k_blk, w_mat, u_mat = block_item
        feed_rows = jnp.concatenate([u_mat, jnp.zeros_like(u_mat)], axis=1) - matmul(
            w_mat, pair_state
        )
        outputs = matmul(q_blk, pair_state) + matmul(visible_scores(q_blk, k_blk), feed_rows)
        return (pair_state + matmul(k_blk.T, feed_rows), outputs)

    final_pair, outputs = lax.scan(
        advance, start_pair(head_width), (q_blocks, k_blocks, w_blocks, u_blocks)
    )
    outputs = outputs.reshape(-1, 2 * head_width)
    return (
        final_pair[:, head_width:],
        final_pair[:, :head_width],
        outputs[:, :head_width],
        outputs[:, head_width:],
    )


def per_device(queries, keys, values, initial_state):
    q_heads, k_heads, v_heads = (
        lax.all_to_all(queries, "head", split_axis=1, concat_axis=0, tiled=True),
        lax.all_to_all(keys, "head", split_axis=1, concat_axis=0, tiled=True),
        lax.all_to_all(values, "head", split_axis=1, concat_axis=0, tiled=True),
    )
    head_width = q_heads.shape[2]
    local_heads = q_heads.shape[1]
    blocks = q_heads.shape[0] // BLOCK
    q_blocks = jnp.moveaxis(q_heads.astype(jnp.float32), 1, 0).reshape(
        local_heads, blocks, BLOCK, head_width
    )
    k_blocks = jnp.moveaxis(unit_rows(k_heads), 1, 0).reshape(local_heads, blocks, -1, head_width)
    v_blocks = jnp.moveaxis(v_heads.astype(jnp.float32), 1, 0).reshape(
        local_heads, blocks, -1, head_width
    )
    w_blocks, u_blocks = all_factors(k_blocks, v_blocks)
    transition, additive, local_out, query_gain = jax.vmap(carried_pass)(
        q_blocks, k_blocks, w_blocks, u_blocks
    )
    at_first = lax.axis_index("seq") == 0
    start_state = jnp.where(at_first, initial_state, jnp.zeros_like(initial_state))

    def relay_step(loop_step, current):
        passed = shifted(batched(transition, current) + additive, "seq", 1)
        return jnp.where(at_first, initial_state, passed)

    incoming = lax.fori_loop(0, lax.axis_size("seq") - 1, relay_step, start_state)
    raw_out = local_out + batched(query_gain, incoming)
    scaled = raw_out * lax.rsqrt(jnp.mean(raw_out * raw_out, axis=-1, keepdims=True) + 1e-06)
    tokens_major = jnp.moveaxis(scaled.astype(jnp.bfloat16), 0, 1)
    return lax.all_to_all(tokens_major, "head", split_axis=0, concat_axis=1, tiled=True)


def solution(mesh):
    placed = (
        P(("seq", "head"), None, None),
        P(("seq", "head"), None, None, None),
        P(("seq", "head"), None, None, None),
        P("head", None, None),
    )
    devices = mesh.shape["seq"] * mesh.shape["head"]

    def chosen(queries, keys, values, initial_state):
        own_heads, width = initial_state.shape[:2]
        inbox = devices * 2 * width * width * 4
        if own_heads == mesh.shape["seq"] and inbox <= INBOX_BYTES:
            return owned_per_device(queries, keys, values, initial_state)
        return per_device(queries, keys, values, initial_state)

    return jax.shard_map(
        chosen,
        mesh=mesh,
        in_specs=placed,
        out_specs=P(("seq", "head"), None, None),
        check_vma=False,
    )
```

```python
import functools

import jax
import jax.numpy as jnp
from jax import lax
from jax.experimental import pallas as pl
from jax.experimental.pallas import tpu as pltpu
from jax.sharding import PartitionSpec as P

BLOCK = 64
BASE = 16
HEADS_A_STEP = 4
INBOX_BYTES = 24 << 20
VMEM_BYTES = 56 << 20

F32 = jnp.float32
BF16 = jnp.bfloat16
MESH = pl.DeviceIdType.MESH


def mm(left, right, dims=((1,), (0,))):
    return lax.dot_general(left, right, (dims, ((), ())), preferred_element_type=F32)


def split(x):
    high = x.astype(BF16)
    return high, (x - high.astype(F32)).astype(BF16)


def cat(parts, axis):
    return jnp.concatenate(parts, axis=axis)


def exact_left(left, right):
    high, low = split(right)
    return mm(cat([left, left], 1), cat([high, low], 0))


def exact_right(left, right):
    high, low = split(left)
    return mm(cat([high, low], 1), cat([right, right], 0))


def both_split(lh, ll, rh, rl):
    return mm(cat([lh, ll], 1), cat([rh, rh], 0)) + mm(lh, rl)


def both(left, right):
    return both_split(*split(left), *split(right))


def odd_rows(x, size):
    rows = x.shape[0]
    return cat([x[s : s + size] for s in range(size, rows, 2 * size)], 0)


def merge_rows(even_from, odd, size):
    rows = even_from.shape[0]
    parts = []
    for i, s in enumerate(range(0, rows, 2 * size)):
        parts += [even_from[s : s + size], odd[i * size : (i + 1) * size]]
    return cat(parts, 0)


def unit_lower_inverses(xs):
    n = xs[0].shape[0]
    row = lax.broadcasted_iota(jnp.int32, (n, n), 0)
    col = lax.broadcasted_iota(jnp.int32, (n, n), 1)
    same = row // BASE == col // BASE
    sub = lax.broadcasted_iota(jnp.int32, (BASE, n), 0)
    lane = lax.broadcasted_iota(jnp.int32, (BASE, n), 1)
    packs = []
    for x in xs:
        inner = jnp.where(same, x, 0.0)
        packed = inner[:BASE]
        for s in range(BASE, n, BASE):
            packed = packed + inner[s : s + BASE]
        packs.append(packed)
    invs = [jnp.where(sub == lane % BASE, 1.0, 0.0) for _ in xs]
    for j in range(BASE - 1):
        at = lane - lane % BASE + j
        coefs = [jnp.take_along_axis(packed, at, axis=1) for packed in packs]
        invs = [inv - coef * inv[j : j + 1] for inv, coef in zip(invs, coefs)]
    ms = [jnp.where(same, cat([inv] * (n // BASE), 0), 0.0) for inv in invs]
    size = BASE
    while size < n:
        near = col // size == row // size - 1
        belows = [split(odd_rows(jnp.where(near, x, 0.0), size)) for x in xs]
        halves = [split(m) for m in ms]
        ys = [both_split(*below, *half) for below, half in zip(belows, halves)]
        ys = [split(merge_rows(jnp.zeros((n, n), F32), y, size)) for y in ys]
        zs = [
            both_split(odd_rows(mh, size), odd_rows(ml, size), *y)
            for (mh, ml), y in zip(halves, ys)
        ]
        ms = [merge_rows(m, odd_rows(m, size) - z, size) for m, z in zip(ms, zs)]
        size *= 2
    return ms


def block_factors(blocks):
    n, width = blocks[0][1].shape
    tokens = blocks[0][0].shape[0]
    row = lax.broadcasted_iota(jnp.int32, (n, n), 0)
    col = lax.broadcasted_iota(jnp.int32, (n, n), 1)
    trow = lax.broadcasted_iota(jnp.int32, (tokens, n), 0)
    tcol = lax.broadcasted_iota(jnp.int32, (tokens, n), 1)
    visible = tcol < (trow + 1) * (n // tokens)
    kqs = [cat([k, q], 0) for q, k, _ in blocks]
    products = [mm(kq, k, ((1,), (1,))) for kq, (_, k, _) in zip(kqs, blocks)]
    xs, d_cols, d_rows, seens = [], [], [], []
    for gs in products:
        gram = gs[:n]
        diag = jnp.where(row == col, gram, 0.0)
        d_col = lax.rsqrt(jnp.sum(diag, axis=1, keepdims=True) + 1e-06)
        d_row = lax.rsqrt(jnp.sum(diag, axis=0, keepdims=True) + 1e-06)
        xs.append(jnp.where(col < row, (2.0 * d_col) * gram * d_row, 0.0))
        d_cols.append(d_col)
        d_rows.append(d_row)
        seens.append(split(jnp.where(visible, gs[n:], 0.0)))
    scaled = [m * (2.0 * d_col) for m, d_col in zip(unit_lower_inverses(xs), d_cols)]
    feds = [exact_right(m, v) for m, (_, _, v) in zip(scaled, blocks)]
    nears = [split(m * d_row) for m, d_row in zip(scaled, d_rows)]
    return kqs, nears, feds, seens


def local_maps(q_ref, k_ref, v_ref, local_ref, gain_ref, first):
    heads, tokens, width = q_ref.shape
    per_token = k_ref.shape[1] // tokens
    step = min(BLOCK, tokens)
    n = step * per_token
    count = tokens // step
    blocks = [
        (
            q_ref[h, b * step : (b + 1) * step],
            k_ref[h, b * n : (b + 1) * n],
            v_ref[h, b * n : (b + 1) * n],
        )
        for b in range(count)
        for h in range(heads)
    ]
    kqs, nears, feds, seens = block_factors(blocks)
    row = lax.broadcasted_iota(jnp.int32, (width, width), 0)
    col = lax.broadcasted_iota(jnp.int32, (width, width), 1)
    eye = jnp.where(row == col, 1.0, 0.0)
    pairs = [cat([jnp.zeros((width, width), F32), eye], 1)] * heads
    for b in range(count):
        at = slice(b * heads, (b + 1) * heads)
        if b == 0:
            qs = [kq[n:].astype(F32) for kq in kqs[at]]
            passed = [cat([jnp.zeros_like(q), q], 1) for q in qs]
            feeds = [
                cat([fed, -mm(cat(list(near), 1), cat([kq[:n], kq[:n]], 0))], 1)
                for fed, near, kq in zip(feds[at], nears[at], kqs[at])
            ]
        else:
            aheads = [exact_left(kq, pair) for kq, pair in zip(kqs[at], pairs)]
            passed = [ahead[n:] for ahead in aheads]
            feeds = [
                cat([fed, jnp.zeros_like(fed)], 1) - both_split(*near, *split(ahead[:n]))
                for fed, near, ahead in zip(feds[at], nears[at], aheads)
            ]
        feeds = [split(feed) for feed in feeds]
        pairs = [
            pair + mm(cat([kq[:n], kq[:n]], 0), cat(list(feed), 0), ((0,), (0,)))
            for pair, kq, feed in zip(pairs, kqs[at], feeds)
        ]
        outs = [
            base + both_split(*seen, *feed)
            for base, seen, feed in zip(passed, seens[at], feeds)
        ]
        for h, out in enumerate(outs):
            local_ref[first + h, b * step : (b + 1) * step] = out[:, :width]
            gain_ref[first + h, b * step : (b + 1) * step] = out[:, width:]
    return pairs


def group_of(step, ns, nh, size):
    own = (lax.axis_index("head") * ns + lax.axis_index("seq")) // size
    groups = ns * nh // size
    return lax.rem(own + 1 + step, groups)


def mixer_kernel(
    ns,
    nh,
    q_ref,
    k_ref,
    v_ref,
    init_ref,
    out_ref,
    local,
    gain,
    t_out,
    a_out,
    t_box,
    a_box,
    states,
    incoming,
    t_send,
    a_send,
    t_recv,
    a_recv,
    s_send,
    s_recv,
):
    size, tokens, width = q_ref.shape
    step = pl.program_id(0)
    si, zi = lax.axis_index("seq"), lax.axis_index("head")
    me = si * nh + zi
    n = ns * nh
    mine = zi * ns + si

    def place(p):
        return p // nh, lax.rem(p, nh)

    def owner(head):
        return lax.rem(head, ns), head // ns

    def map_copies(head):
        return [
            pltpu.make_async_remote_copy(
                src_ref=src.at[head],
                dst_ref=box.at[me],
                send_sem=send.at[head],
                recv_sem=recv.at[me],
                device_id=owner(head),
                device_id_type=MESH,
            )
            for src, box, send, recv in (
                (t_out, t_box, t_send, t_recv),
                (a_out, a_box, a_send, a_recv),
            )
        ]

    def state_copy(d):
        return pltpu.make_async_remote_copy(
            src_ref=states.at[d],
            dst_ref=incoming.at[mine],
            send_sem=s_send.at[d],
            recv_sem=s_recv.at[mine],
            device_id=place(d),
            device_id_type=MESH,
        )

    @pl.when(step == 0)
    def _():
        barrier = pltpu.get_barrier_semaphore()

        @pl.loop(1, n)
        def _(i):
            pl.semaphore_signal(
                barrier, inc=1, device_id=place(lax.rem(me + i, n)), device_id_type=MESH
            )

        pl.semaphore_wait(barrier, n - 1)

    first = group_of(step, ns, nh, size) * size
    pairs = local_maps(q_ref, k_ref, v_ref, local, gain, first)
    for h, pair in enumerate(pairs):
        t_out[first + h] = pair[:, width:]
        a_out[first + h] = pair[:, :width].astype(a_out.dtype)

    @pl.loop(first, first + size)
    def _(head):
        @pl.when(head != mine)
        def _():
            for copy in map_copies(head):
                copy.start()

        @pl.when(head == mine)
        def _():
            pltpu.make_async_copy(t_out.at[mine], t_box.at[me], t_recv.at[me]).start()
            pltpu.make_async_copy(a_out.at[mine], a_box.at[me], a_recv.at[me]).start()

    @pl.when(step == pl.num_programs(0) - 1)
    def _():
        def advance(d, state):
            states[d] = state.astype(states.dtype)

            @pl.when(d != me)
            def _():
                state_copy(d).start()

            @pl.when(d == me)
            def _():
                pltpu.make_async_copy(
                    states.at[d], incoming.at[mine], s_recv.at[mine]
                ).start()

            pltpu.make_async_copy(t_box.at[d], t_box.at[d], t_recv.at[d]).wait()
            pltpu.make_async_copy(a_box.at[d], a_box.at[d], a_recv.at[d]).wait()
            return both(t_box[d], state) + a_box[d].astype(F32)

        lax.fori_loop(0, n, advance, init_ref[si])

        @pl.loop(0, n // size)
        def _(g):
            heads = [g * size + h for h in range(size)]
            for head in heads:
                pltpu.make_async_copy(
                    incoming.at[head], incoming.at[head], s_recv.at[head]
                ).wait()
            for head in heads:
                raw = local[head] + exact_right(gain[head], incoming[head])
                mean = jnp.mean(raw * raw, axis=-1, keepdims=True)
                out_ref[head] = (raw * lax.rsqrt(mean + 1e-06)).astype(out_ref.dtype)

        @pl.loop(0, n)
        def _(head):
            @pl.when(head != mine)
            def _():
                for copy in map_copies(head):
                    copy.wait_send()

            @pl.when(head != me)
            def _():
                state_copy(head).wait_send()


def mixer(q, k, v, initial_state):
    ns, nh = lax.axis_size("seq"), lax.axis_size("head")
    heads, tokens, width = q.shape
    g = HEADS_A_STEP

    def spec(rows):
        return pl.BlockSpec((g, rows, width), lambda i: (group_of(i, ns, nh, g), 0, 0))

    square = (heads, width, width)
    return pl.pallas_call(
        functools.partial(mixer_kernel, ns, nh),
        grid=(heads // g,),
        in_specs=[
            spec(tokens),
            spec(k.shape[1]),
            spec(k.shape[1]),
            pl.BlockSpec(initial_state.shape, lambda i: (0, 0, 0)),
        ],
        out_specs=pl.BlockSpec((heads, tokens, width), lambda i: (0, 0, 0)),
        out_shape=jax.ShapeDtypeStruct((heads, tokens, width), BF16),
        scratch_shapes=[
            pltpu.VMEM((heads, tokens, width), F32),
            pltpu.VMEM((heads, tokens, width), F32),
            pltpu.VMEM(square, F32),
            pltpu.VMEM(square, BF16),
            pltpu.VMEM(square, F32),
            pltpu.VMEM(square, BF16),
            pltpu.VMEM(square, BF16),
            pltpu.VMEM(square, BF16),
        ]
        + [pltpu.SemaphoreType.DMA((heads,))] * 6,
        compiler_params=pltpu.CompilerParams(
            collective_id=0, has_side_effects=True, vmem_limit_bytes=VMEM_BYTES
        ),
        name="mixer",
    )(q, k, v, initial_state)


def owned_per_device(queries, keys, values, initial_state):
    tokens, heads, width = queries.shape
    q = jnp.swapaxes(queries, 0, 1)
    k = jnp.moveaxis(keys, 1, 0).reshape(heads, -1, width)
    v = jnp.moveaxis(values, 1, 0).reshape(heads, -1, width)
    return jnp.swapaxes(mixer(q, k, v, initial_state), 0, 1)


HIGH = lax.Precision.HIGHEST


def shifted(value, axis, by):
    size = lax.axis_size(axis)
    pairs = [(i, i + by) for i in range(size) if 0 <= i + by < size]
    return lax.ppermute(value, axis, pairs)


def matmul(left, right):
    return jnp.dot(left, right, precision=HIGH, preferred_element_type=jnp.float32)


def batched(left, right):
    return jnp.einsum("hij,hjk->hik", left, right, precision=HIGH)


def unit_rows(raw_keys):
    floats = raw_keys.astype(jnp.float32)
    return floats * lax.rsqrt(jnp.sum(floats * floats, axis=-1, keepdims=True) + 1e-06)


def all_factors(k_blocks, v_blocks):
    updates = k_blocks.shape[2]
    head_width = k_blocks.shape[3]
    gram = jnp.einsum("hbid,hbjd->hbij", k_blocks, k_blocks, precision=HIGH)
    system = jnp.eye(updates, dtype=jnp.float32) + jnp.tril(2.0 * gram, -1)
    solved = lax.linalg.triangular_solve(
        system,
        2.0 * jnp.concatenate([k_blocks, v_blocks], axis=-1),
        left_side=True,
        lower=True,
        unit_diagonal=True,
    )
    return (solved[..., :head_width], solved[..., head_width:])


def visible_scores(q_blk, k_blk):
    rows = q_blk.shape[0]
    updates = k_blk.shape[0]
    per_token = updates // rows
    row_ids = lax.broadcasted_iota(jnp.int32, (rows, updates), 0)
    col_ids = lax.broadcasted_iota(jnp.int32, (rows, updates), 1)
    return jnp.where(col_ids < (row_ids + 1) * per_token, matmul(q_blk, k_blk.T), 0.0)


def start_pair(head_width):
    return jnp.concatenate(
        [jnp.zeros((head_width, head_width), jnp.float32), jnp.eye(head_width, dtype=jnp.float32)],
        axis=1,
    )


def carried_pass(q_blocks, k_blocks, w_blocks, u_blocks):
    head_width = q_blocks.shape[2]

    def advance(pair_state, block_item):
        q_blk, k_blk, w_mat, u_mat = block_item
        feed_rows = jnp.concatenate([u_mat, jnp.zeros_like(u_mat)], axis=1) - matmul(
            w_mat, pair_state
        )
        outputs = matmul(q_blk, pair_state) + matmul(visible_scores(q_blk, k_blk), feed_rows)
        return (pair_state + matmul(k_blk.T, feed_rows), outputs)

    final_pair, outputs = lax.scan(
        advance, start_pair(head_width), (q_blocks, k_blocks, w_blocks, u_blocks)
    )
    outputs = outputs.reshape(-1, 2 * head_width)
    return (
        final_pair[:, head_width:],
        final_pair[:, :head_width],
        outputs[:, :head_width],
        outputs[:, head_width:],
    )


def per_device(queries, keys, values, initial_state):
    q_heads, k_heads, v_heads = (
        lax.all_to_all(queries, "head", split_axis=1, concat_axis=0, tiled=True),
        lax.all_to_all(keys, "head", split_axis=1, concat_axis=0, tiled=True),
        lax.all_to_all(values, "head", split_axis=1, concat_axis=0, tiled=True),
    )
    head_width = q_heads.shape[2]
    local_heads = q_heads.shape[1]
    blocks = q_heads.shape[0] // BLOCK
    q_blocks = jnp.moveaxis(q_heads.astype(jnp.float32), 1, 0).reshape(
        local_heads, blocks, BLOCK, head_width
    )
    k_blocks = jnp.moveaxis(unit_rows(k_heads), 1, 0).reshape(local_heads, blocks, -1, head_width)
    v_blocks = jnp.moveaxis(v_heads.astype(jnp.float32), 1, 0).reshape(
        local_heads, blocks, -1, head_width
    )
    w_blocks, u_blocks = all_factors(k_blocks, v_blocks)
    transition, additive, local_out, query_gain = jax.vmap(carried_pass)(
        q_blocks, k_blocks, w_blocks, u_blocks
    )
    at_first = lax.axis_index("seq") == 0
    start_state = jnp.where(at_first, initial_state, jnp.zeros_like(initial_state))

    def relay_step(loop_step, current):
        passed = shifted(batched(transition, current) + additive, "seq", 1)
        return jnp.where(at_first, initial_state, passed)

    incoming = lax.fori_loop(0, lax.axis_size("seq") - 1, relay_step, start_state)
    raw_out = local_out + batched(query_gain, incoming)
    scaled = raw_out * lax.rsqrt(jnp.mean(raw_out * raw_out, axis=-1, keepdims=True) + 1e-06)
    tokens_major = jnp.moveaxis(scaled.astype(jnp.bfloat16), 0, 1)
    return lax.all_to_all(tokens_major, "head", split_axis=0, concat_axis=1, tiled=True)


def solution(mesh):
    placed = (
        P(("seq", "head"), None, None),
        P(("seq", "head"), None, None, None),
        P(("seq", "head"), None, None, None),
        P("head", None, None),
    )
    devices = mesh.shape["seq"] * mesh.shape["head"]

    def chosen(queries, keys, values, initial_state):
        own_heads, width = initial_state.shape[:2]
        inbox = devices * 2 * width * width * 4
        if own_heads == mesh.shape["seq"] and inbox <= INBOX_BYTES:
            return owned_per_device(queries, keys, values, initial_state)
        return per_device(queries, keys, values, initial_state)

    return jax.shard_map(
        chosen,
        mesh=mesh,
        in_specs=placed,
        out_specs=P(("seq", "head"), None, None),
        check_vma=False,
    )
```

```python
import functools

import jax
import jax.numpy as jnp
from jax import lax
from jax.experimental import pallas as pl
from jax.experimental.pallas import tpu as pltpu
from jax.sharding import PartitionSpec as P

BLOCK = 64
BASE = 16
HEADS_A_STEP = 8
INBOX_BYTES = 24 << 20
VMEM_BYTES = 56 << 20

F32 = jnp.float32
BF16 = jnp.bfloat16
MESH = pl.DeviceIdType.MESH


def mm(left, right, dims=((1,), (0,))):
    return lax.dot_general(left, right, (dims, ((), ())), preferred_element_type=F32)


def split(x):
    high = x.astype(BF16)
    return high, (x - high.astype(F32)).astype(BF16)


def cat(parts, axis):
    return jnp.concatenate(parts, axis=axis)


def exact_left(left, right):
    high, low = split(right)
    return mm(cat([left, left], 1), cat([high, low], 0))


def exact_right(left, right):
    high, low = split(left)
    return mm(cat([high, low], 1), cat([right, right], 0))


def both_split(lh, ll, rh, rl):
    return mm(cat([lh, ll], 1), cat([rh, rh], 0)) + mm(lh, rl)


def both(left, right):
    return both_split(*split(left), *split(right))


def odd_rows(x, size):
    rows = x.shape[0]
    return cat([x[s : s + size] for s in range(size, rows, 2 * size)], 0)


def merge_rows(even_from, odd, size):
    rows = even_from.shape[0]
    parts = []
    for i, s in enumerate(range(0, rows, 2 * size)):
        parts += [even_from[s : s + size], odd[i * size : (i + 1) * size]]
    return cat(parts, 0)


def unit_lower_inverses(xs):
    n = xs[0].shape[0]
    row = lax.broadcasted_iota(jnp.int32, (n, n), 0)
    col = lax.broadcasted_iota(jnp.int32, (n, n), 1)
    same = row // BASE == col // BASE
    sub = lax.broadcasted_iota(jnp.int32, (BASE, n), 0)
    lane = lax.broadcasted_iota(jnp.int32, (BASE, n), 1)
    packs = []
    for x in xs:
        inner = jnp.where(same, x, 0.0)
        packed = inner[:BASE]
        for s in range(BASE, n, BASE):
            packed = packed + inner[s : s + BASE]
        packs.append(packed)
    invs = [jnp.where(sub == lane % BASE, 1.0, 0.0) for _ in xs]
    for j in range(BASE - 1):
        at = lane - lane % BASE + j
        coefs = [jnp.take_along_axis(packed, at, axis=1) for packed in packs]
        invs = [inv - coef * inv[j : j + 1] for inv, coef in zip(invs, coefs)]
    ms = [jnp.where(same, cat([inv] * (n // BASE), 0), 0.0) for inv in invs]
    size = BASE
    while size < n:
        near = col // size == row // size - 1
        belows = [split(odd_rows(jnp.where(near, x, 0.0), size)) for x in xs]
        halves = [split(m) for m in ms]
        ys = [both_split(*below, *half) for below, half in zip(belows, halves)]
        ys = [split(merge_rows(jnp.zeros((n, n), F32), y, size)) for y in ys]
        zs = [
            both_split(odd_rows(mh, size), odd_rows(ml, size), *y)
            for (mh, ml), y in zip(halves, ys)
        ]
        ms = [merge_rows(m, odd_rows(m, size) - z, size) for m, z in zip(ms, zs)]
        size *= 2
    return ms


def block_factors(blocks):
    n, width = blocks[0][1].shape
    tokens = blocks[0][0].shape[0]
    row = lax.broadcasted_iota(jnp.int32, (n, n), 0)
    col = lax.broadcasted_iota(jnp.int32, (n, n), 1)
    trow = lax.broadcasted_iota(jnp.int32, (tokens, n), 0)
    tcol = lax.broadcasted_iota(jnp.int32, (tokens, n), 1)
    visible = tcol < (trow + 1) * (n // tokens)
    kqs = [cat([k, q], 0) for q, k, _ in blocks]
    products = [mm(kq, k, ((1,), (1,))) for kq, (_, k, _) in zip(kqs, blocks)]
    xs, d_cols, d_rows, seens = [], [], [], []
    for gs in products:
        gram = gs[:n]
        diag = jnp.where(row == col, gram, 0.0)
        d_col = lax.rsqrt(jnp.sum(diag, axis=1, keepdims=True) + 1e-06)
        d_row = lax.rsqrt(jnp.sum(diag, axis=0, keepdims=True) + 1e-06)
        xs.append(jnp.where(col < row, (2.0 * d_col) * gram * d_row, 0.0))
        d_cols.append(d_col)
        d_rows.append(d_row)
        seens.append(split(jnp.where(visible, gs[n:], 0.0)))
    scaled = [m * (2.0 * d_col) for m, d_col in zip(unit_lower_inverses(xs), d_cols)]
    feds = [exact_right(m, v) for m, (_, _, v) in zip(scaled, blocks)]
    nears = [split(m * d_row) for m, d_row in zip(scaled, d_rows)]
    return kqs, nears, feds, seens


def local_maps(q_ref, k_ref, v_ref, local_ref, gain_ref, first):
    heads, tokens, width = q_ref.shape
    per_token = k_ref.shape[2]
    step = min(BLOCK, tokens)
    n = step * per_token
    count = tokens // step
    blocks = [
        (
            q_ref[h, b * step : (b + 1) * step],
            k_ref[b * step : (b + 1) * step, h].reshape(n, width),
            v_ref[b * step : (b + 1) * step, h].reshape(n, width),
        )
        for b in range(count)
        for h in range(heads)
    ]
    kqs, nears, feds, seens = block_factors(blocks)
    row = lax.broadcasted_iota(jnp.int32, (width, width), 0)
    col = lax.broadcasted_iota(jnp.int32, (width, width), 1)
    eye = jnp.where(row == col, 1.0, 0.0)
    pairs = [cat([jnp.zeros((width, width), F32), eye], 1)] * heads
    for b in range(count):
        at = slice(b * heads, (b + 1) * heads)
        if b == 0:
            qs = [kq[n:].astype(F32) for kq in kqs[at]]
            passed = [cat([jnp.zeros_like(q), q], 1) for q in qs]
            feeds = [
                cat([fed, -mm(cat(list(near), 1), cat([kq[:n], kq[:n]], 0))], 1)
                for fed, near, kq in zip(feds[at], nears[at], kqs[at])
            ]
        else:
            aheads = [exact_left(kq, pair) for kq, pair in zip(kqs[at], pairs)]
            passed = [ahead[n:] for ahead in aheads]
            feeds = [
                cat([fed, jnp.zeros_like(fed)], 1) - both_split(*near, *split(ahead[:n]))
                for fed, near, ahead in zip(feds[at], nears[at], aheads)
            ]
        feeds = [split(feed) for feed in feeds]
        pairs = [
            pair + mm(cat([kq[:n], kq[:n]], 0), cat(list(feed), 0), ((0,), (0,)))
            for pair, kq, feed in zip(pairs, kqs[at], feeds)
        ]
        outs = [
            base + both_split(*seen, *feed)
            for base, seen, feed in zip(passed, seens[at], feeds)
        ]
        for h, out in enumerate(outs):
            local_ref[first + h, b * step : (b + 1) * step] = out[:, :width]
            gain_ref[first + h, b * step : (b + 1) * step] = out[:, width:]
    return pairs


def group_of(step, ns, nh, size):
    own = (lax.axis_index("head") * ns + lax.axis_index("seq")) // size
    groups = ns * nh // size
    return lax.rem(own + 1 + step, groups)


def mixer_kernel(
    ns,
    nh,
    q_ref,
    k_ref,
    v_ref,
    init_ref,
    out_ref,
    local,
    gain,
    t_out,
    a_out,
    t_box,
    a_box,
    states,
    incoming,
    t_send,
    a_send,
    t_recv,
    a_recv,
    s_send,
    s_recv,
):
    size, tokens, width = q_ref.shape
    step = pl.program_id(0)
    si, zi = lax.axis_index("seq"), lax.axis_index("head")
    me = si * nh + zi
    n = ns * nh
    mine = zi * ns + si

    def place(p):
        return p // nh, lax.rem(p, nh)

    def owner(head):
        return lax.rem(head, ns), head // ns

    def map_copies(head):
        return [
            pltpu.make_async_remote_copy(
                src_ref=src.at[head],
                dst_ref=box.at[me],
                send_sem=send.at[head],
                recv_sem=recv.at[me],
                device_id=owner(head),
                device_id_type=MESH,
            )
            for src, box, send, recv in (
                (t_out, t_box, t_send, t_recv),
                (a_out, a_box, a_send, a_recv),
            )
        ]

    def state_copy(d):
        return pltpu.make_async_remote_copy(
            src_ref=states.at[d],
            dst_ref=incoming.at[mine],
            send_sem=s_send.at[d],
            recv_sem=s_recv.at[mine],
            device_id=place(d),
            device_id_type=MESH,
        )

    @pl.when(step == 0)
    def _():
        barrier = pltpu.get_barrier_semaphore()

        @pl.loop(1, n)
        def _(i):
            pl.semaphore_signal(
                barrier, inc=1, device_id=place(lax.rem(me + i, n)), device_id_type=MESH
            )

        pl.semaphore_wait(barrier, n - 1)

    first = group_of(step, ns, nh, size) * size
    pairs = local_maps(q_ref, k_ref, v_ref, local, gain, first)
    for h, pair in enumerate(pairs):
        t_out[first + h] = pair[:, width:]
        a_out[first + h] = pair[:, :width].astype(a_out.dtype)

    @pl.loop(first, first + size)
    def _(head):
        @pl.when(head != mine)
        def _():
            for copy in map_copies(head):
                copy.start()

        @pl.when(head == mine)
        def _():
            pltpu.make_async_copy(t_out.at[mine], t_box.at[me], t_recv.at[me]).start()
            pltpu.make_async_copy(a_out.at[mine], a_box.at[me], a_recv.at[me]).start()

    @pl.when(step == pl.num_programs(0) - 1)
    def _():
        def advance(d, state):
            states[d] = state.astype(states.dtype)

            @pl.when(d != me)
            def _():
                state_copy(d).start()

            @pl.when(d == me)
            def _():
                pltpu.make_async_copy(
                    states.at[d], incoming.at[mine], s_recv.at[mine]
                ).start()

            pltpu.make_async_copy(t_box.at[d], t_box.at[d], t_recv.at[d]).wait()
            pltpu.make_async_copy(a_box.at[d], a_box.at[d], a_recv.at[d]).wait()
            return both(t_box[d], state) + a_box[d].astype(F32)

        lax.fori_loop(0, n, advance, init_ref[si])

        @pl.loop(0, n // size)
        def _(g):
            heads = [g * size + h for h in range(size)]
            for head in heads:
                pltpu.make_async_copy(
                    incoming.at[head], incoming.at[head], s_recv.at[head]
                ).wait()
            for head in heads:
                raw = local[head] + exact_right(gain[head], incoming[head])
                mean = jnp.mean(raw * raw, axis=-1, keepdims=True)
                out_ref[head] = (raw * lax.rsqrt(mean + 1e-06)).astype(out_ref.dtype)

        @pl.loop(0, n)
        def _(head):
            @pl.when(head != mine)
            def _():
                for copy in map_copies(head):
                    copy.wait_send()

            @pl.when(head != me)
            def _():
                state_copy(head).wait_send()


def mixer(q, k, v, initial_state):
    ns, nh = lax.axis_size("seq"), lax.axis_size("head")
    heads, tokens, width = q.shape
    g = HEADS_A_STEP

    def spec(rows):
        return pl.BlockSpec((g, rows, width), lambda i: (group_of(i, ns, nh, g), 0, 0))

    def by_token(rows):
        return pl.BlockSpec(
            (tokens, g, rows, width), lambda i: (0, group_of(i, ns, nh, g), 0, 0)
        )

    square = (heads, width, width)
    return pl.pallas_call(
        functools.partial(mixer_kernel, ns, nh),
        grid=(heads // g,),
        in_specs=[
            spec(tokens),
            by_token(k.shape[2]),
            by_token(k.shape[2]),
            pl.BlockSpec(initial_state.shape, lambda i: (0, 0, 0)),
        ],
        out_specs=pl.BlockSpec((heads, tokens, width), lambda i: (0, 0, 0)),
        out_shape=jax.ShapeDtypeStruct((heads, tokens, width), BF16),
        scratch_shapes=[
            pltpu.VMEM((heads, tokens, width), F32),
            pltpu.VMEM((heads, tokens, width), F32),
            pltpu.VMEM(square, F32),
            pltpu.VMEM(square, BF16),
            pltpu.VMEM(square, F32),
            pltpu.VMEM(square, BF16),
            pltpu.VMEM(square, BF16),
            pltpu.VMEM(square, BF16),
        ]
        + [pltpu.SemaphoreType.DMA((heads,))] * 6,
        compiler_params=pltpu.CompilerParams(
            collective_id=0, has_side_effects=True, vmem_limit_bytes=VMEM_BYTES
        ),
        name="mixer",
    )(q, k, v, initial_state)


def owned_per_device(queries, keys, values, initial_state):
    tokens, heads, width = queries.shape
    q = jnp.swapaxes(queries, 0, 1)
    return jnp.swapaxes(mixer(q, keys, values, initial_state), 0, 1)


HIGH = lax.Precision.HIGHEST


def shifted(value, axis, by):
    size = lax.axis_size(axis)
    pairs = [(i, i + by) for i in range(size) if 0 <= i + by < size]
    return lax.ppermute(value, axis, pairs)


def matmul(left, right):
    return jnp.dot(left, right, precision=HIGH, preferred_element_type=jnp.float32)


def batched(left, right):
    return jnp.einsum("hij,hjk->hik", left, right, precision=HIGH)


def unit_rows(raw_keys):
    floats = raw_keys.astype(jnp.float32)
    return floats * lax.rsqrt(jnp.sum(floats * floats, axis=-1, keepdims=True) + 1e-06)


def all_factors(k_blocks, v_blocks):
    updates = k_blocks.shape[2]
    head_width = k_blocks.shape[3]
    gram = jnp.einsum("hbid,hbjd->hbij", k_blocks, k_blocks, precision=HIGH)
    system = jnp.eye(updates, dtype=jnp.float32) + jnp.tril(2.0 * gram, -1)
    solved = lax.linalg.triangular_solve(
        system,
        2.0 * jnp.concatenate([k_blocks, v_blocks], axis=-1),
        left_side=True,
        lower=True,
        unit_diagonal=True,
    )
    return (solved[..., :head_width], solved[..., head_width:])


def visible_scores(q_blk, k_blk):
    rows = q_blk.shape[0]
    updates = k_blk.shape[0]
    per_token = updates // rows
    row_ids = lax.broadcasted_iota(jnp.int32, (rows, updates), 0)
    col_ids = lax.broadcasted_iota(jnp.int32, (rows, updates), 1)
    return jnp.where(col_ids < (row_ids + 1) * per_token, matmul(q_blk, k_blk.T), 0.0)


def start_pair(head_width):
    return jnp.concatenate(
        [jnp.zeros((head_width, head_width), jnp.float32), jnp.eye(head_width, dtype=jnp.float32)],
        axis=1,
    )


def carried_pass(q_blocks, k_blocks, w_blocks, u_blocks):
    head_width = q_blocks.shape[2]

    def advance(pair_state, block_item):
        q_blk, k_blk, w_mat, u_mat = block_item
        feed_rows = jnp.concatenate([u_mat, jnp.zeros_like(u_mat)], axis=1) - matmul(
            w_mat, pair_state
        )
        outputs = matmul(q_blk, pair_state) + matmul(visible_scores(q_blk, k_blk), feed_rows)
        return (pair_state + matmul(k_blk.T, feed_rows), outputs)

    final_pair, outputs = lax.scan(
        advance, start_pair(head_width), (q_blocks, k_blocks, w_blocks, u_blocks)
    )
    outputs = outputs.reshape(-1, 2 * head_width)
    return (
        final_pair[:, head_width:],
        final_pair[:, :head_width],
        outputs[:, :head_width],
        outputs[:, head_width:],
    )


def per_device(queries, keys, values, initial_state):
    q_heads, k_heads, v_heads = (
        lax.all_to_all(queries, "head", split_axis=1, concat_axis=0, tiled=True),
        lax.all_to_all(keys, "head", split_axis=1, concat_axis=0, tiled=True),
        lax.all_to_all(values, "head", split_axis=1, concat_axis=0, tiled=True),
    )
    head_width = q_heads.shape[2]
    local_heads = q_heads.shape[1]
    blocks = q_heads.shape[0] // BLOCK
    q_blocks = jnp.moveaxis(q_heads.astype(jnp.float32), 1, 0).reshape(
        local_heads, blocks, BLOCK, head_width
    )
    k_blocks = jnp.moveaxis(unit_rows(k_heads), 1, 0).reshape(local_heads, blocks, -1, head_width)
    v_blocks = jnp.moveaxis(v_heads.astype(jnp.float32), 1, 0).reshape(
        local_heads, blocks, -1, head_width
    )
    w_blocks, u_blocks = all_factors(k_blocks, v_blocks)
    transition, additive, local_out, query_gain = jax.vmap(carried_pass)(
        q_blocks, k_blocks, w_blocks, u_blocks
    )
    at_first = lax.axis_index("seq") == 0
    start_state = jnp.where(at_first, initial_state, jnp.zeros_like(initial_state))

    def relay_step(loop_step, current):
        passed = shifted(batched(transition, current) + additive, "seq", 1)
        return jnp.where(at_first, initial_state, passed)

    incoming = lax.fori_loop(0, lax.axis_size("seq") - 1, relay_step, start_state)
    raw_out = local_out + batched(query_gain, incoming)
    scaled = raw_out * lax.rsqrt(jnp.mean(raw_out * raw_out, axis=-1, keepdims=True) + 1e-06)
    tokens_major = jnp.moveaxis(scaled.astype(jnp.bfloat16), 0, 1)
    return lax.all_to_all(tokens_major, "head", split_axis=0, concat_axis=1, tiled=True)


def solution(mesh):
    placed = (
        P(("seq", "head"), None, None),
        P(("seq", "head"), None, None, None),
        P(("seq", "head"), None, None, None),
        P("head", None, None),
    )
    devices = mesh.shape["seq"] * mesh.shape["head"]

    def chosen(queries, keys, values, initial_state):
        own_heads, width = initial_state.shape[:2]
        inbox = devices * 2 * width * width * 4
        if own_heads == mesh.shape["seq"] and inbox <= INBOX_BYTES:
            return owned_per_device(queries, keys, values, initial_state)
        return per_device(queries, keys, values, initial_state)

    return jax.shard_map(
        chosen,
        mesh=mesh,
        in_specs=placed,
        out_specs=P(("seq", "head"), None, None),
        check_vma=False,
    )
```
